256 devices in a mesh: dp: 4 (over y), ep: 32 (over x, z), tp: 2 (over core).
Axes of the slice: x: 4, y: 4, z: 8, core: 2. Of those that a mesh axis runs over, the one named last changes fastest.
Arguments:
- grad_out: bfloat16 [16384, 4096], P(('dp', 'ep'), 'tp'), may hold values from -6 to 6
- hidden: bfloat16 [16384, 8, 768], P(('dp', 'ep'), None, 'tp'), may hold values from -0.29882812 to 0.29882812
- gates: bfloat16 [16384, 8], P(('dp', 'ep')), may hold values from 0.019897461 to 0.29882812
- expert_ids: int32 [16384, 8], P(('dp', 'ep')), may hold values from 0 to 63, all different within a row; in each aligned block of 128 rows (0 to 127, 128 to 255, ...) at most 24 rows name the same one
- down_weight: bfloat16 [64, 768, 4096], P('ep', 'tp'), may hold values from -0.09375 to 0.09375
Outputs:
- d_hidden: bfloat16 [16384, 8, 768], P(('dp', 'ep'), None, 'tp')
- d_gates: bfloat16 [16384, 8], P(('dp', 'ep'))
- d_weight: bfloat16 [64, 768, 4096], P('ep', 'tp', 'dp')
The draws below stay inside these ranges and needn't reach their ends.
Inputs may be any that keep to these rules, and one draw needn't show every extreme that they name: `expert_ids`: in each aligned block of 128 rows (the tokens of one index of dp and ep taken together), no expert is named by more than 24 rows, a bound that some block reaches; the 8 experts of a token differ.
All inputs are finite; a program needn't handle non-finite values.
Results may differ from the reference program's by a relative error of at most 0.0049.
Values may be sent and summed in bfloat16 or wider, within the bound.
A program may use at most 256 MiB of HBM per device.

```python
import math
import jax
import jax.numpy as jnp
import numpy as np
from jax import lax

D = 4096
FFW = 768
TOPK = 8
TOK_DEV = 128
EXPERTS = 64
CAP = 24
TOKENS = 16384
N_DP = 4
N_EP = 32


def shard_levels(own_key, extent, split, smallest, largest):
    def one(position, blocks):
        draws = jax.random.uniform(jax.random.fold_in(jax.random.fold_in(own_key, 6), position), (blocks,), jnp.float32, smallest / len(split), largest / len(split))
        return jnp.repeat(jnp.exp(draws), extent[position] // blocks).reshape((-1,) + (1,) * (len(extent) - position - 1))

    factor_of = one(*split[0])
    for cut in split[1:]:
        factor_of = factor_of * one(*cut)
    return factor_of


def shared_out(stream_key, own, number, rows, count, top, limit, slope):
    ranking = jax.random.permutation(stream_key, count)
    heavy_load, ordinary = load_shares(count, rows * top, limit, slope, True), load_shares(count, rows * top, limit, slope, False)
    places = jnp.arange(count)

    def named(sizes, turn):
        used = int((sizes > 0).sum())
        fixed = max(1, used // 4)
        passed = fixed + (places - fixed + turn * (used - fixed)) % max(1, count - fixed)
        return jnp.zeros((count,), jnp.int32).at[ranking[jnp.where(places < fixed, places, passed)]].set(jnp.asarray(sizes, jnp.int32))

    sizes = jnp.where(number % 4 == 0, named(heavy_load, number // 4), named(ordinary, number - number // 4 - 1))
    mixed = jax.random.permutation(jax.random.fold_in(own, 3), count)
    giver, receiver = mixed[0:count // 2 * 2:2], mixed[1:count // 2 * 2:2]
    slack = jnp.minimum(sizes[giver] - 1, limit - sizes[receiver]) // 2
    slack = jnp.where((giver == ranking[0]) | (receiver == ranking[0]) | (sizes[receiver] == 0), 0, jnp.maximum(slack, 0))
    passed = jax.random.randint(jax.random.fold_in(own, 4), (count // 2,), 0, 1 << 20) % (slack + 1)
    sizes = sizes.at[giver].add(-passed).at[receiver].add(passed)
    items = jnp.searchsorted(jnp.cumsum(sizes), jnp.arange(rows * top), side="right").astype(jnp.int32)
    table = items.reshape(top, rows).T
    table = table[jax.random.permutation(jax.random.fold_in(own, 1), rows)]
    turn = jax.random.randint(jax.random.fold_in(own, 2), (rows, 1), 0, top)
    return jnp.take_along_axis(table, (jnp.arange(top)[None, :] + turn) % top, axis=1)


def load_shares(number_of, total, reach, slope, full):
    portions = [(1 << 20) // math.isqrt(rank ** slope) + 1 for rank in range(1, number_of + 1)]
    largest = reach if full else min(reach, max(-(-total // number_of), total * portions[0] // sum(portions)))
    least = 1 if total - largest >= number_of - 1 else 0
    counts, spare = [largest] + [least] * (number_of - 1), total - largest - least * (number_of - 1)
    while spare > 0:
        free = [i for i in range(1, number_of) if counts[i] < largest] or [i for i in range(1, number_of) if counts[i] < reach]
        whole, remaining = sum([portions[i] for i in free]), spare
        for i in free:
            extra = min(reach - counts[i], max(1, remaining * portions[i] // whole), spare)
            counts[i] = counts[i] + extra
            spare = spare - extra
    return np.array(counts)


def normal_values(key, shape, scale, bound, split=(), kind=jnp.bfloat16):
    values = scale * jax.random.normal(key, shape, jnp.float32)
    if split:
        values = values * shard_levels(key, shape, split, -0.22, 0.18)
    return jnp.clip(values, -bound, bound).astype(kind)


def setup_inputs(seed: int = 0) -> dict:
    splits = jax.random.split(jax.random.key(seed), 6)
    grad_out = normal_values(splits[0], (TOKENS, D), 1.0, 6.0, ((0, 128), (1, 2)))
    hidden = normal_values(splits[1], (TOKENS, TOPK, FFW), 0.05, 0.29882812, ((0, 128), (2, 2)))
    gates = jnp.clip(0.019897461 + 0.27893066 * jax.random.uniform(splits[2], (TOKENS, TOPK), jnp.float32) ** shard_levels(splits[2], (TOKENS, TOPK), ((0, 128),), -0.2, 0.2), 0.019897461, 0.29882812).astype(jnp.bfloat16)
    expert_ids_keys = jax.random.split(jax.random.fold_in(splits[3], 1), TOKENS // TOK_DEV)
    expert_ids_turns = jax.random.permutation(jax.random.fold_in(splits[3], 3), TOKENS // TOK_DEV)
    expert_ids = jax.vmap(lambda own, number: shared_out(jax.random.fold_in(splits[3], 2), own, number, TOK_DEV, EXPERTS, TOPK, CAP, 2))(expert_ids_keys, expert_ids_turns).reshape((TOKENS, TOPK))
    down_weight = normal_values(splits[4], (EXPERTS, FFW, D), D ** -0.5, 0.09375, ((0, 32), (1, 2)))
    return dict(grad_out=grad_out, hidden=hidden, gates=gates, expert_ids=expert_ids, down_weight=down_weight)


def rank_rows(block_ids):
    one_hot = (block_ids[:, None] == jnp.arange(EXPERTS, dtype=jnp.int32)[None, :]).astype(jnp.int32)
    return jnp.sum((jnp.cumsum(one_hot, axis=0) - 1) * one_hot, axis=1).astype(jnp.int32)


def reference(grad_out, hidden, gates, expert_ids, down_weight):
    block_count = N_DP * N_EP
    pair_count = TOK_DEV * TOPK
    all_pairs = block_count * pair_count
    block_ids = expert_ids.reshape(block_count, pair_count)
    rank_in = lax.map(rank_rows, block_ids)
    block_no = jnp.arange(block_count, dtype=jnp.int32)[:, None]
    column = (block_no * CAP + rank_in).reshape(-1).astype(jnp.int32)
    pair_no = jnp.arange(all_pairs, dtype=jnp.int32)
    flat_ids = expert_ids.reshape(-1).astype(jnp.int32)
    table = jnp.full((EXPERTS, block_count * CAP), all_pairs, jnp.int32).at[flat_ids, column].set(pair_no)
    hid_flat = hidden.reshape(all_pairs, FFW)
    gate_flat = gates.reshape(all_pairs)

    def per_expert(inputs):
        slot_rows, weight = inputs
        filled = slot_rows < all_pairs
        safe_idx = jnp.where(filled, slot_rows, 0).astype(jnp.int32)
        dy_rows = jnp.where(filled[:, None], grad_out[safe_idx // TOPK], jnp.zeros((), grad_out.dtype)).astype(grad_out.dtype)
        hid_rows = jnp.where(filled[:, None], hid_flat[safe_idx], jnp.zeros((), hidden.dtype)).astype(hidden.dtype)
        gate_rows = jnp.where(filled, gate_flat[safe_idx], jnp.zeros((), gates.dtype)).astype(jnp.float32)
        back_proj = jnp.dot(dy_rows, weight.T, preferred_element_type=jnp.float32)
        d_rows = (gate_rows[:, None] * back_proj).astype(jnp.bfloat16)
        dg_rows = jnp.sum(back_proj * hid_rows.astype(jnp.float32), axis=1).astype(jnp.bfloat16)
        scaled = (gate_rows[:, None] * hid_rows.astype(jnp.float32)).astype(jnp.bfloat16)
        d_mat = jnp.dot(scaled.T, dy_rows, preferred_element_type=jnp.float32).astype(jnp.bfloat16)
        return d_rows, dg_rows, d_mat

    dh_all, dg_all, d_weight = lax.map(per_expert, (table, down_weight))
    flat_table = table.reshape(-1)
    d_hidden = jnp.zeros((all_pairs + 1, FFW), jnp.bfloat16).at[flat_table].set(dh_all.reshape(-1, FFW))
    d_gates = jnp.zeros((all_pairs + 1,), jnp.bfloat16).at[flat_table].set(dg_all.reshape(-1))
    d_hidden = d_hidden[:all_pairs].reshape(TOKENS, TOPK, FFW)
    d_gates = d_gates[:all_pairs].reshape(TOKENS, TOPK)
    return d_hidden, d_gates, d_weight
```

```python
import jax
import jax.numpy as jnp
from jax import lax
from jax.sharding import PartitionSpec as P


def shards(grad_out, hidden, gates, expert_ids, down_weight):
    ep_size = lax.axis_size("ep")
    experts_here, hidden_part, model_width = down_weight.shape
    experts_all = ep_size * experts_here
    tok_count, top_count = expert_ids.shape
    capacity = min(tok_count, 3 * tok_count * top_count // (2 * experts_all))
    pair_count = tok_count * top_count
    slot_count = experts_here * capacity
    slots_all = experts_all * capacity
    f32, bf16 = jnp.float32, jnp.bfloat16

    expert_iota = jnp.arange(experts_all, dtype=jnp.int32)
    pair_hot = expert_ids[:, :, None] == expert_iota[None, None, :]
    tok_has = jnp.any(pair_hot, axis=1).astype(bf16)
    tok_iota = lax.optimization_barrier(jnp.arange(tok_count, dtype=jnp.int32))
    earlier = (tok_iota[None, :] < tok_iota[:, None]).astype(bf16)
    before = jnp.dot(earlier, tok_has, preferred_element_type=f32)
    rank_in = jnp.sum(jnp.where(pair_hot, before[:, None, :], 0.0), axis=2).astype(jnp.int32)
    slot_of = (expert_ids * capacity + rank_in).reshape(pair_count)

    slot_iota = lax.optimization_barrier(jnp.arange(slots_all, dtype=jnp.int32))
    sel_pair = (slot_iota[:, None] == slot_of[None, :]).astype(bf16)
    sel_tok = jnp.sum(sel_pair.reshape(slots_all, tok_count, top_count), axis=2)

    chosen = jnp.dot(sel_tok, grad_out, preferred_element_type=f32).astype(bf16)
    hid_rows = jnp.dot(
        sel_pair, hidden.reshape(pair_count, hidden_part), preferred_element_type=f32
    ).astype(bf16)
    gate_rows = jnp.dot(
        sel_pair, gates.reshape(pair_count, 1), preferred_element_type=f32
    ).astype(bf16)

    half_recv = lax.all_to_all(
        chosen.reshape(ep_size, slot_count, grad_out.shape[1]),
        "ep",
        split_axis=0,
        concat_axis=0,
        tiled=True,
    )
    hid_recv = lax.all_to_all(
        hid_rows.reshape(ep_size, slot_count, hidden_part), "ep", split_axis=0, concat_axis=0, tiled=True
    )
    gate_recv = lax.all_to_all(
        gate_rows.reshape(ep_size, slot_count), "ep", split_axis=0, concat_axis=0, tiled=True
    )
    dy_recv = lax.all_gather(half_recv, "tp", axis=2, tiled=True)
    dy_slots = dy_recv.reshape(ep_size, experts_here, capacity, model_width)
    hid_slots = hid_recv.reshape(ep_size, experts_here, capacity, hidden_part)
    gate_slots = gate_recv.reshape(ep_size, experts_here, capacity).astype(f32)

    scaled = (gate_slots[..., None] * hid_slots.astype(f32)).astype(bf16)
    weight_term = jnp.einsum("secf,secd->efd", scaled, dy_slots, preferred_element_type=f32)
    d_weight = lax.psum_scatter(
        weight_term.astype(bf16), "dp", scatter_dimension=2, tiled=True
    )

    back_proj = jnp.einsum(
        "secd,efd->secf", dy_slots, down_weight, preferred_element_type=f32
    )
    partial_value = jnp.sum(back_proj * hid_slots.astype(f32), axis=3)
    dot_total = lax.psum(partial_value, "tp")
    send_dh = (
        (gate_slots[..., None] * back_proj)
        .astype(bf16)
        .reshape(ep_size, slot_count, hidden_part)
    )
    send_dg = dot_total.astype(bf16).reshape(ep_size, slot_count)
    got_dh, got_dg = (
        lax.all_to_all(send_dh, "ep", split_axis=0, concat_axis=0, tiled=True),
        lax.all_to_all(send_dg, "ep", split_axis=0, concat_axis=0, tiled=True),
    )
    d_hidden = (
        jnp.dot(sel_pair.T, got_dh.reshape(slots_all, hidden_part), preferred_element_type=f32)
        .astype(bf16)
        .reshape(tok_count, top_count, hidden_part)
    )
    d_gates = (
        jnp.dot(sel_pair.T, got_dg.reshape(slots_all, 1), preferred_element_type=f32)
        .astype(bf16)
        .reshape(tok_count, top_count)
    )
    return (d_hidden, d_gates, d_weight)


def solution(mesh):
    placed = (
        P(("dp", "ep"), "tp"),
        P(("dp", "ep"), None, "tp"),
        P(("dp", "ep"), None),
        P(("dp", "ep"), None),
        P("ep", "tp", None),
    )
    return jax.shard_map(
        shards,
        mesh=mesh,
        in_specs=placed,
        out_specs=(P(("dp", "ep"), None, "tp"), P(("dp", "ep"), None), P("ep", "tp", "dp")),
        check_vma=False,
    )
```

```python
import jax
import jax.numpy as jnp
from jax import lax
from jax.sharding import PartitionSpec as P


def shards(grad_out, hidden, gates, expert_ids, down_weight):
    ep_size = lax.axis_size("ep")
    experts_here, hidden_part, model_width = down_weight.shape
    experts_all = ep_size * experts_here
    tok_count, top_count = expert_ids.shape
    capacity = min(tok_count, 3 * tok_count * top_count // (2 * experts_all))
    pair_count = tok_count * top_count
    slot_count = experts_here * capacity
    slots_all = experts_all * capacity
    f32, bf16 = jnp.float32, jnp.bfloat16

    expert_iota = jnp.arange(experts_all, dtype=jnp.int32)
    pair_hot = expert_ids[:, :, None] == expert_iota[None, None, :]
    tok_has = jnp.any(pair_hot, axis=1).astype(bf16)
    tok_iota = lax.optimization_barrier(jnp.arange(tok_count, dtype=jnp.int32))
    earlier = (tok_iota[None, :] < tok_iota[:, None]).astype(bf16)
    before = jnp.dot(earlier, tok_has, preferred_element_type=f32)
    rank_in = jnp.sum(jnp.where(pair_hot, before[:, None, :], 0.0), axis=2).astype(jnp.int32)
    slot_of = (expert_ids * capacity + rank_in).reshape(pair_count)

    slot_iota = lax.optimization_barrier(jnp.arange(slots_all, dtype=jnp.int32))
    sel_pair = (slot_iota[:, None] == slot_of[None, :]).astype(bf16)
    pair_iota = lax.optimization_barrier(jnp.arange(pair_count, dtype=jnp.int32))
    tok_of_pair = (pair_iota[:, None] // top_count == tok_iota[None, :]).astype(bf16)
    sel_tok = jnp.dot(sel_pair, tok_of_pair, preferred_element_type=f32).astype(bf16)

    chosen = jnp.dot(sel_tok, grad_out, preferred_element_type=f32).astype(bf16)
    hid_rows = jnp.dot(
        sel_pair, hidden.reshape(pair_count, hidden_part), preferred_element_type=f32
    ).astype(bf16)
    gate_rows = jnp.dot(
        sel_pair, gates.reshape(pair_count, 1), preferred_element_type=f32
    ).astype(bf16)

    half_recv = lax.all_to_all(
        chosen.reshape(ep_size, slot_count, grad_out.shape[1]),
        "ep",
        split_axis=0,
        concat_axis=0,
        tiled=True,
    )
    flat_hid = slot_count * hidden_part
    both = jnp.concatenate(
        [hid_rows.reshape(ep_size, flat_hid), gate_rows.reshape(ep_size, slot_count)], axis=1
    )
    both_recv = lax.all_to_all(both, "ep", split_axis=0, concat_axis=0, tiled=True)
    hid_recv = both_recv[:, :flat_hid]
    gate_recv = both_recv[:, flat_hid:]
    dy_recv = lax.all_gather(half_recv, "tp", axis=2, tiled=True)
    dy_slots = dy_recv.reshape(ep_size, experts_here, capacity, model_width)
    hid_slots = hid_recv.reshape(ep_size, experts_here, capacity, hidden_part)
    gate_slots = gate_recv.reshape(ep_size, experts_here, capacity).astype(f32)

    scaled = (gate_slots[..., None] * hid_slots.astype(f32)).astype(bf16)
    weight_term = jnp.einsum("secf,secd->efd", scaled, dy_slots, preferred_element_type=f32)
    d_weight = lax.psum_scatter(
        weight_term.astype(bf16), "dp", scatter_dimension=2, tiled=True
    )

    back_proj = jnp.einsum(
        "secd,efd->secf", dy_slots, down_weight, preferred_element_type=f32
    )
    partial_value = jnp.sum(back_proj * hid_slots.astype(f32), axis=3)
    dot_total = lax.psum(partial_value, "tp")
    send_dh = (
        (gate_slots[..., None] * back_proj)
        .astype(bf16)
        .reshape(ep_size, slot_count, hidden_part)
    )
    send_dg = dot_total.astype(bf16).reshape(ep_size, slot_count)
    back = jnp.concatenate([send_dh.reshape(ep_size, flat_hid), send_dg], axis=1)
    got = lax.all_to_all(back, "ep", split_axis=0, concat_axis=0, tiled=True)
    got_dh = got[:, :flat_hid]
    got_dg = got[:, flat_hid:]
    d_hidden = (
        jnp.dot(sel_pair.T, got_dh.reshape(slots_all, hidden_part), preferred_element_type=f32)
        .astype(bf16)
        .reshape(tok_count, top_count, hidden_part)
    )
    d_gates = (
        jnp.dot(sel_pair.T, got_dg.reshape(slots_all, 1), preferred_element_type=f32)
        .astype(bf16)
        .reshape(tok_count, top_count)
    )
    return (d_hidden, d_gates, d_weight)


def solution(mesh):
    placed = (
        P(("dp", "ep"), "tp"),
        P(("dp", "ep"), None, "tp"),
        P(("dp", "ep"), None),
        P(("dp", "ep"), None),
        P("ep", "tp", None),
    )
    return jax.shard_map(
        shards,
        mesh=mesh,
        in_specs=placed,
        out_specs=(P(("dp", "ep"), None, "tp"), P(("dp", "ep"), None), P("ep", "tp", "dp")),
        check_vma=False,
    )
```

```python
import jax
import jax.numpy as jnp
from jax import lax
from jax.sharding import PartitionSpec as P


def shards(grad_out, hidden, gates, expert_ids, down_weight):
    ep_size = lax.axis_size("ep")
    experts_here, hidden_part, model_width = down_weight.shape
    experts_all = ep_size * experts_here
    tok_count, top_count = expert_ids.shape
    capacity = min(tok_count, 3 * tok_count * top_count // (2 * experts_all))
    pair_count = tok_count * top_count
    slot_count = experts_here * capacity
    slots_all = experts_all * capacity
    f32, bf16 = jnp.float32, jnp.bfloat16

    expert_iota = jnp.arange(experts_all, dtype=jnp.int32)
    pair_hot = expert_ids[:, :, None] == expert_iota[None, None, :]
    tok_has = jnp.any(pair_hot, axis=1).astype(bf16)
    tok_iota = lax.optimization_barrier(jnp.arange(tok_count, dtype=jnp.int32))
    earlier = (tok_iota[None, :] < tok_iota[:, None]).astype(bf16)
    before = jnp.dot(earlier, tok_has, preferred_element_type=f32)
    rank_in = jnp.sum(jnp.where(pair_hot, before[:, None, :], 0.0), axis=2).astype(jnp.int32)
    slot_of = (expert_ids * capacity + rank_in).reshape(pair_count)

    slot_iota = lax.optimization_barrier(jnp.arange(slots_all, dtype=jnp.int32))
    sel_pair = (slot_iota[:, None] == slot_of[None, :]).astype(bf16)

    hid_rows = jnp.dot(
        sel_pair, hidden.reshape(pair_count, hidden_part), preferred_element_type=f32
    ).astype(bf16)
    gate_rows = jnp.dot(
        sel_pair, gates.reshape(pair_count, 1), preferred_element_type=f32
    ).astype(bf16)

    ids_all = lax.all_gather(expert_ids, "ep")
    grad_all = lax.all_gather(grad_out, "ep")
    own = lax.axis_index("ep") * experts_here + jnp.arange(experts_here, dtype=jnp.int32)
    has_own = jnp.any(ids_all[:, :, :, None] == own[None, None, None, :], axis=2)
    has_own_b = has_own.astype(bf16)
    before_own = jnp.einsum("ts,bsl->btl", earlier, has_own_b, preferred_element_type=f32)
    rank_iota = jnp.arange(capacity, dtype=jnp.int32)
    pick = (
        has_own[:, :, :, None]
        & (before_own.astype(jnp.int32)[:, :, :, None] == rank_iota[None, None, None, :])
    ).astype(bf16)
    half_recv = (
        jnp.einsum("btlr,btd->blrd", pick, grad_all, preferred_element_type=f32)
        .astype(bf16)
        .reshape(ep_size, slot_count, grad_out.shape[1])
    )
    flat_hid = slot_count * hidden_part
    both = jnp.concatenate(
        [hid_rows.reshape(ep_size, flat_hid), gate_rows.reshape(ep_size, slot_count)], axis=1
    )
    both_recv = lax.all_to_all(both, "ep", split_axis=0, concat_axis=0, tiled=True)
    hid_recv = both_recv[:, :flat_hid]
    gate_recv = both_recv[:, flat_hid:]
    dy_recv = lax.all_gather(half_recv, "tp", axis=2, tiled=True)
    dy_slots = dy_recv.reshape(ep_size, experts_here, capacity, model_width)
    hid_slots = hid_recv.reshape(ep_size, experts_here, capacity, hidden_part)
    gate_slots = gate_recv.reshape(ep_size, experts_here, capacity).astype(f32)

    scaled = (gate_slots[..., None] * hid_slots.astype(f32)).astype(bf16)
    weight_term = jnp.einsum("secf,secd->efd", scaled, dy_slots, preferred_element_type=f32)
    d_weight = lax.psum_scatter(
        weight_term.astype(bf16), "dp", scatter_dimension=2, tiled=True
    )

    back_proj = jnp.einsum(
        "secd,efd->secf", dy_slots, down_weight, preferred_element_type=f32
    )
    partial_value = jnp.sum(back_proj * hid_slots.astype(f32), axis=3)
    dot_total = lax.psum(partial_value, "tp")
    send_dh = (
        (gate_slots[..., None] * back_proj)
        .astype(bf16)
        .reshape(ep_size, slot_count, hidden_part)
    )
    send_dg = dot_total.astype(bf16).reshape(ep_size, slot_count)
    back = jnp.concatenate([send_dh.reshape(ep_size, flat_hid), send_dg], axis=1)
    got = lax.all_to_all(back, "ep", split_axis=0, concat_axis=0, tiled=True)
    got_dh = got[:, :flat_hid]
    got_dg = got[:, flat_hid:]
    d_hidden = (
        jnp.dot(sel_pair.T, got_dh.reshape(slots_all, hidden_part), preferred_element_type=f32)
        .astype(bf16)
        .reshape(tok_count, top_count, hidden_part)
    )
    d_gates = (
        jnp.dot(sel_pair.T, got_dg.reshape(slots_all, 1), preferred_element_type=f32)
        .astype(bf16)
        .reshape(tok_count, top_count)
    )
    return (d_hidden, d_gates, d_weight)


def solution(mesh):
    placed = (
        P(("dp", "ep"), "tp"),
        P(("dp", "ep"), None, "tp"),
        P(("dp", "ep"), None),
        P(("dp", "ep"), None),
        P("ep", "tp", None),
    )
    return jax.shard_map(
        shards,
        mesh=mesh,
        in_specs=placed,
        out_specs=(P(("dp", "ep"), None, "tp"), P(("dp", "ep"), None), P("ep", "tp", "dp")),
        check_vma=False,
    )
```

```python
import jax
import jax.numpy as jnp
from jax import lax
from jax.sharding import PartitionSpec as P


def shards(grad_out, hidden, gates, expert_ids, down_weight):
    ep_size = lax.axis_size("ep")
    experts_here, hidden_part, model_width = down_weight.shape
    experts_all = ep_size * experts_here
    tok_count, top_count = expert_ids.shape
    capacity = min(tok_count, 3 * tok_count * top_count // (2 * experts_all))
    pair_count = tok_count * top_count
    slot_count = experts_here * capacity
    slots_all = experts_all * capacity
    f32, bf16 = jnp.float32, jnp.bfloat16

    expert_iota = jnp.arange(experts_all, dtype=jnp.int32)
    pair_hot = expert_ids[:, :, None] == expert_iota[None, None, :]
    tok_has = jnp.any(pair_hot, axis=1).astype(bf16)
    tok_iota = lax.optimization_barrier(jnp.arange(tok_count, dtype=jnp.int32))
    earlier = (tok_iota[None, :] < tok_iota[:, None]).astype(bf16)
    before = jnp.dot(earlier, tok_has, preferred_element_type=f32)
    rank_in = jnp.sum(jnp.where(pair_hot, before[:, None, :], 0.0), axis=2).astype(jnp.int32)
    slot_of = (expert_ids * capacity + rank_in).reshape(pair_count)

    slot_iota = lax.optimization_barrier(jnp.arange(slots_all, dtype=jnp.int32))
    sel_pair = (slot_iota[:, None] == slot_of[None, :]).astype(bf16)

    pair_iota = lax.optimization_barrier(jnp.arange(pair_count, dtype=jnp.int32))
    tok_of_pair = (pair_iota[:, None] // top_count == tok_iota[None, :]).astype(bf16)
    sel_tok = jnp.dot(sel_pair, tok_of_pair, preferred_element_type=f32).astype(bf16)
    slot_tok = jnp.dot(
        sel_tok, (tok_iota + 1).astype(bf16)[:, None], preferred_element_type=f32
    ).astype(bf16)
    hid_rows = jnp.dot(
        sel_pair, hidden.reshape(pair_count, hidden_part), preferred_element_type=f32
    ).astype(bf16)
    gate_rows = jnp.dot(
        sel_pair, gates.reshape(pair_count, 1), preferred_element_type=f32
    ).astype(bf16)

    width = grad_out.shape[1]
    split = width // 2
    chosen = jnp.dot(sel_tok, grad_out[:, :split], preferred_element_type=f32).astype(bf16)
    grad_all = lax.all_gather(grad_out[:, split:], "ep")

    flat_hid = slot_count * hidden_part
    both = jnp.concatenate(
        [
            hid_rows.reshape(ep_size, flat_hid),
            gate_rows.reshape(ep_size, slot_count),
            slot_tok.reshape(ep_size, slot_count),
        ],
        axis=1,
    )
    both_recv = lax.all_to_all(both, "ep", split_axis=0, concat_axis=0, tiled=True)
    hid_recv = both_recv[:, :flat_hid]
    gate_recv = both_recv[:, flat_hid : flat_hid + slot_count]
    tok_recv = both_recv[:, flat_hid + slot_count :].astype(jnp.int32)

    first_recv = lax.all_to_all(
        chosen.reshape(ep_size, slot_count, split), "ep", split_axis=0, concat_axis=0, tiled=True
    )
    pick = (tok_recv[:, :, None] == (tok_iota + 1)[None, None, :]).astype(bf16)
    rest_recv = jnp.einsum("bst,btd->bsd", pick, grad_all, preferred_element_type=f32).astype(bf16)
    half_recv = jnp.concatenate([first_recv, rest_recv], axis=2)
    dy_recv = lax.all_gather(half_recv, "tp", axis=2, tiled=True)
    dy_slots = dy_recv.reshape(ep_size, experts_here, capacity, model_width)
    hid_slots = hid_recv.reshape(ep_size, experts_here, capacity, hidden_part)
    gate_slots = gate_recv.reshape(ep_size, experts_here, capacity).astype(f32)

    scaled = (gate_slots[..., None] * hid_slots.astype(f32)).astype(bf16)
    weight_term = jnp.einsum("secf,secd->efd", scaled, dy_slots, preferred_element_type=f32)
    d_weight = lax.psum_scatter(
        weight_term.astype(bf16), "dp", scatter_dimension=2, tiled=True
    )

    back_proj = jnp.einsum(
        "secd,efd->secf", dy_slots, down_weight, preferred_element_type=f32
    )
    partial_value = jnp.sum(back_proj * hid_slots.astype(f32), axis=3)
    dot_total = lax.psum(partial_value, "tp")
    send_dh = (
        (gate_slots[..., None] * back_proj)
        .astype(bf16)
        .reshape(ep_size, slot_count, hidden_part)
    )
    send_dg = dot_total.astype(bf16).reshape(ep_size, slot_count)
    back = jnp.concatenate([send_dh.reshape(ep_size, flat_hid), send_dg], axis=1)
    got = lax.all_to_all(back, "ep", split_axis=0, concat_axis=0, tiled=True)
    got_dh = got[:, :flat_hid]
    got_dg = got[:, flat_hid:]
    d_hidden = (
        jnp.dot(sel_pair.T, got_dh.reshape(slots_all, hidden_part), preferred_element_type=f32)
        .astype(bf16)
        .reshape(tok_count, top_count, hidden_part)
    )
    d_gates = (
        jnp.dot(sel_pair.T, got_dg.reshape(slots_all, 1), preferred_element_type=f32)
        .astype(bf16)
        .reshape(tok_count, top_count)
    )
    return (d_hidden, d_gates, d_weight)


def solution(mesh):
    placed = (
        P(("dp", "ep"), "tp"),
        P(("dp", "ep"), None, "tp"),
        P(("dp", "ep"), None),
        P(("dp", "ep"), None),
        P("ep", "tp", None),
    )
    return jax.shard_map(
        shards,
        mesh=mesh,
        in_specs=placed,
        out_specs=(P(("dp", "ep"), None, "tp"), P(("dp", "ep"), None), P("ep", "tp", "dp")),
        check_vma=False,
    )
```

```python
import jax
import jax.numpy as jnp
from jax import lax
from jax.sharding import PartitionSpec as P


def shards(grad_out, hidden, gates, expert_ids, down_weight):
    ep_size = lax.axis_size("ep")
    experts_here, hidden_part, model_width = down_weight.shape
    experts_all = ep_size * experts_here
    tok_count, top_count = expert_ids.shape
    capacity = min(tok_count, 3 * tok_count * top_count // (2 * experts_all))
    pair_count = tok_count * top_count
    slot_count = experts_here * capacity
    slots_all = experts_all * capacity
    f32, bf16 = jnp.float32, jnp.bfloat16

    expert_iota = jnp.arange(experts_all, dtype=jnp.int32)
    pair_hot = expert_ids[:, :, None] == expert_iota[None, None, :]
    tok_has = jnp.any(pair_hot, axis=1).astype(bf16)
    tok_iota = lax.optimization_barrier(jnp.arange(tok_count, dtype=jnp.int32))
    earlier = (tok_iota[None, :] < tok_iota[:, None]).astype(bf16)
    before = jnp.dot(earlier, tok_has, preferred_element_type=f32)
    rank_in = jnp.sum(jnp.where(pair_hot, before[:, None, :], 0.0), axis=2).astype(jnp.int32)
    slot_of = (expert_ids * capacity + rank_in).reshape(pair_count)

    slot_iota = lax.optimization_barrier(jnp.arange(slots_all, dtype=jnp.int32))
    sel_pair = (slot_iota[:, None] == slot_of[None, :]).astype(bf16)

    pair_iota = lax.optimization_barrier(jnp.arange(pair_count, dtype=jnp.int32))
    tok_of_pair = (pair_iota[:, None] // top_count == tok_iota[None, :]).astype(bf16)
    sel_tok = jnp.dot(sel_pair, tok_of_pair, preferred_element_type=f32).astype(bf16)
    slot_tok = jnp.dot(
        sel_tok, (tok_iota + 1).astype(bf16)[:, None], preferred_element_type=f32
    ).astype(bf16)
    hid_rows = jnp.dot(
        sel_pair, hidden.reshape(pair_count, hidden_part), preferred_element_type=f32
    ).astype(bf16)
    gate_rows = jnp.dot(
        sel_pair, gates.reshape(pair_count, 1), preferred_element_type=f32
    ).astype(bf16)

    grad_all = lax.all_gather(grad_out, "ep")

    flat_hid = slot_count * hidden_part
    both = jnp.concatenate(
        [
            hid_rows.reshape(ep_size, flat_hid),
            gate_rows.reshape(ep_size, slot_count),
            slot_tok.reshape(ep_size, slot_count),
        ],
        axis=1,
    )
    both_recv = lax.all_to_all(both, "ep", split_axis=0, concat_axis=0, tiled=True)
    hid_recv = both_recv[:, :flat_hid]
    gate_recv = both_recv[:, flat_hid : flat_hid + slot_count]
    tok_recv = both_recv[:, flat_hid + slot_count :].astype(jnp.int32)

    pick = (tok_recv[:, :, None] == (tok_iota + 1)[None, None, :]).astype(bf16)
    half_recv = jnp.einsum("bst,btd->bsd", pick, grad_all, preferred_element_type=f32).astype(bf16)
    dy_recv = lax.all_gather(half_recv, "tp", axis=2, tiled=True)
    dy_slots = dy_recv.reshape(ep_size, experts_here, capacity, model_width)
    hid_slots = hid_recv.reshape(ep_size, experts_here, capacity, hidden_part)
    gate_slots = gate_recv.reshape(ep_size, experts_here, capacity).astype(f32)

    scaled = (gate_slots[..., None] * hid_slots.astype(f32)).astype(bf16)
    weight_term = jnp.einsum("secf,secd->efd", scaled, dy_slots, preferred_element_type=f32)
    d_weight = lax.psum_scatter(
        weight_term.astype(bf16), "dp", scatter_dimension=2, tiled=True
    )

    back_proj = jnp.einsum(
        "secd,efd->secf", dy_slots, down_weight, preferred_element_type=f32
    )
    partial_value = jnp.sum(back_proj * hid_slots.astype(f32), axis=3)
    dot_total = lax.psum(partial_value, "tp")
    send_dh = (
        (gate_slots[..., None] * back_proj)
        .astype(bf16)
        .reshape(ep_size, slot_count, hidden_part)
    )
    send_dg = dot_total.astype(bf16).reshape(ep_size, slot_count)
    back = jnp.concatenate([send_dh.reshape(ep_size, flat_hid), send_dg], axis=1)
    got = lax.all_to_all(back, "ep", split_axis=0, concat_axis=0, tiled=True)
    got_dh = got[:, :flat_hid]
    got_dg = got[:, flat_hid:]
    d_hidden = (
        jnp.dot(sel_pair.T, got_dh.reshape(slots_all, hidden_part), preferred_element_type=f32)
        .astype(bf16)
        .reshape(tok_count, top_count, hidden_part)
    )
    d_gates = (
        jnp.dot(sel_pair.T, got_dg.reshape(slots_all, 1), preferred_element_type=f32)
        .astype(bf16)
        .reshape(tok_count, top_count)
    )
    return (d_hidden, d_gates, d_weight)


def solution(mesh):
    placed = (
        P(("dp", "ep"), "tp"),
        P(("dp", "ep"), None, "tp"),
        P(("dp", "ep"), None),
        P(("dp", "ep"), None),
        P("ep", "tp", None),
    )
    return jax.shard_map(
        shards,
        mesh=mesh,
        in_specs=placed,
        out_specs=(P(("dp", "ep"), None, "tp"), P(("dp", "ep"), None), P("ep", "tp", "dp")),
        check_vma=False,
    )
```

```python
import jax
import jax.numpy as jnp
from jax import lax
from jax.sharding import PartitionSpec as P


def shards(grad_out, hidden, gates, expert_ids, down_weight):
    ep_size = lax.axis_size("ep")
    experts_here, hidden_part, model_width = down_weight.shape
    experts_all = ep_size * experts_here
    tok_count, top_count = expert_ids.shape
    capacity = min(tok_count, 3 * tok_count * top_count // (2 * experts_all))
    pair_count = tok_count * top_count
    slot_count = experts_here * capacity
    slots_all = experts_all * capacity
    f32, bf16 = jnp.float32, jnp.bfloat16

    expert_iota = jnp.arange(experts_all, dtype=jnp.int32)
    pair_hot = expert_ids[:, :, None] == expert_iota[None, None, :]
    tok_has = jnp.any(pair_hot, axis=1).astype(bf16)
    tok_iota = lax.optimization_barrier(jnp.arange(tok_count, dtype=jnp.int32))
    earlier = (tok_iota[None, :] < tok_iota[:, None]).astype(bf16)
    before = jnp.dot(earlier, tok_has, preferred_element_type=f32)
    rank_in = jnp.sum(jnp.where(pair_hot, before[:, None, :], 0.0), axis=2).astype(jnp.int32)
    slot_of = (expert_ids * capacity + rank_in).reshape(pair_count)

    slot_iota = lax.optimization_barrier(jnp.arange(slots_all, dtype=jnp.int32))
    sel_pair = (slot_iota[:, None] == slot_of[None, :]).astype(bf16)
    pair_iota = lax.optimization_barrier(jnp.arange(pair_count, dtype=jnp.int32))
    tok_of_pair = (pair_iota[:, None] // top_count == tok_iota[None, :]).astype(bf16)
    sel_tok = jnp.dot(sel_pair, tok_of_pair, preferred_element_type=f32).astype(bf16)

    scaled_pairs = (
        gates.astype(f32)[:, :, None] * hidden.astype(f32)
    ).astype(bf16).reshape(pair_count, hidden_part)
    scaled_rows = jnp.dot(sel_pair, scaled_pairs, preferred_element_type=f32).astype(bf16)
    chosen = jnp.dot(sel_tok, grad_out, preferred_element_type=f32).astype(bf16)

    half_recv = lax.all_to_all(
        chosen.reshape(ep_size, slot_count, grad_out.shape[1]),
        "ep",
        split_axis=0,
        concat_axis=0,
        tiled=True,
    )
    scaled_recv = lax.all_to_all(
        scaled_rows.reshape(ep_size, slot_count, hidden_part), "ep", split_axis=0, concat_axis=0, tiled=True
    )
    dy_recv = lax.all_gather(half_recv, "tp", axis=2, tiled=True)
    dy_slots = dy_recv.reshape(ep_size, experts_here, capacity, model_width)
    scaled_slots = scaled_recv.reshape(ep_size, experts_here, capacity, hidden_part)

    weight_term = jnp.einsum("secf,secd->efd", scaled_slots, dy_slots, preferred_element_type=f32)
    d_weight = lax.psum_scatter(
        weight_term.astype(bf16), "dp", scatter_dimension=2, tiled=True
    )

    back_proj = jnp.einsum(
        "secd,efd->secf", dy_slots, down_weight, preferred_element_type=f32
    )
    got_bp = lax.all_to_all(
        back_proj.astype(bf16).reshape(ep_size, slot_count, hidden_part),
        "ep",
        split_axis=0,
        concat_axis=0,
        tiled=True,
    )
    bp_pairs = jnp.dot(
        sel_pair.T, got_bp.reshape(slots_all, hidden_part), preferred_element_type=f32
    ).reshape(tok_count, top_count, hidden_part)
    d_hidden = (gates.astype(f32)[:, :, None] * bp_pairs).astype(bf16)
    part_dot = jnp.sum(bp_pairs * hidden.astype(f32), axis=2)
    d_gates = lax.psum(part_dot, "tp").astype(bf16)
    return (d_hidden, d_gates, d_weight)


def solution(mesh):
    placed = (
        P(("dp", "ep"), "tp"),
        P(("dp", "ep"), None, "tp"),
        P(("dp", "ep"), None),
        P(("dp", "ep"), None),
        P("ep", "tp", None),
    )
    return jax.shard_map(
        shards,
        mesh=mesh,
        in_specs=placed,
        out_specs=(P(("dp", "ep"), None, "tp"), P(("dp", "ep"), None), P("ep", "tp", "dp")),
        check_vma=False,
    )
```

```python
import jax
import jax.numpy as jnp
from jax import lax
from jax.sharding import PartitionSpec as P


def shards(grad_out, hidden, gates, expert_ids, down_weight):
    ep_size = lax.axis_size("ep")
    experts_here, hidden_part, model_width = down_weight.shape
    experts_all = ep_size * experts_here
    tok_count, top_count = expert_ids.shape
    capacity = min(tok_count, 3 * tok_count * top_count // (2 * experts_all))
    pair_count = tok_count * top_count
    slot_count = experts_here * capacity
    slots_all = experts_all * capacity
    f32, bf16 = jnp.float32, jnp.bfloat16

    expert_iota = jnp.arange(experts_all, dtype=jnp.int32)
    pair_hot = expert_ids[:, :, None] == expert_iota[None, None, :]
    tok_has = jnp.any(pair_hot, axis=1).astype(bf16)
    tok_iota = lax.optimization_barrier(jnp.arange(tok_count, dtype=jnp.int32))
    earlier = (tok_iota[None, :] < tok_iota[:, None]).astype(bf16)
    before = jnp.dot(earlier, tok_has, preferred_element_type=f32)
    rank_in = jnp.sum(jnp.where(pair_hot, before[:, None, :], 0.0), axis=2).astype(jnp.int32)
    slot_of = (expert_ids * capacity + rank_in).reshape(pair_count)

    slot_iota = lax.optimization_barrier(jnp.arange(slots_all, dtype=jnp.int32))
    sel_pair = (slot_iota[:, None] == slot_of[None, :]).astype(bf16)
    pair_iota = lax.optimization_barrier(jnp.arange(pair_count, dtype=jnp.int32))
    tok_of_pair = (pair_iota[:, None] // top_count == tok_iota[None, :]).astype(bf16)
    sel_tok = jnp.dot(sel_pair, tok_of_pair, preferred_element_type=f32).astype(bf16)

    scaled_pairs = (
        gates.astype(f32)[:, :, None] * hidden.astype(f32)
    ).astype(bf16).reshape(pair_count, hidden_part)
    scaled_rows = jnp.dot(sel_pair, scaled_pairs, preferred_element_type=f32).astype(bf16)
    chosen = jnp.dot(sel_tok, grad_out, preferred_element_type=f32).astype(bf16)

    half_recv = lax.all_to_all(
        chosen.reshape(ep_size, slot_count, grad_out.shape[1]),
        "ep",
        split_axis=0,
        concat_axis=0,
        tiled=True,
    )
    scaled_recv = lax.all_to_all(
        scaled_rows.reshape(ep_size, slot_count, hidden_part), "ep", split_axis=0, concat_axis=0, tiled=True
    )
    dy_recv = lax.all_gather(half_recv, "tp", axis=2, tiled=True)
    dy_slots = dy_recv.reshape(ep_size, experts_here, capacity, model_width)
    scaled_slots = scaled_recv.reshape(ep_size, experts_here, capacity, hidden_part)

    weight_term = jnp.einsum("secf,secd->efd", scaled_slots, dy_slots, preferred_element_type=f32)
    weight_half = weight_term.astype(bf16)
    d_weight = lax.psum_scatter(weight_half, "dp", scatter_dimension=2, tiled=True)

    dy_after, _ = lax.optimization_barrier((dy_slots, weight_half))
    back_proj = jnp.einsum(
        "secd,efd->secf", dy_after, down_weight, preferred_element_type=f32
    )
    got_bp = lax.all_to_all(
        back_proj.astype(bf16).reshape(ep_size, slot_count, hidden_part),
        "ep",
        split_axis=0,
        concat_axis=0,
        tiled=True,
    )
    bp_pairs = jnp.dot(
        sel_pair.T, got_bp.reshape(slots_all, hidden_part), preferred_element_type=f32
    ).reshape(tok_count, top_count, hidden_part)
    d_hidden = (gates.astype(f32)[:, :, None] * bp_pairs).astype(bf16)
    part_dot = jnp.sum(bp_pairs * hidden.astype(f32), axis=2)
    d_gates = lax.psum(part_dot, "tp").astype(bf16)
    return (d_hidden, d_gates, d_weight)


def solution(mesh):
    placed = (
        P(("dp", "ep"), "tp"),
        P(("dp", "ep"), None, "tp"),
        P(("dp", "ep"), None),
        P(("dp", "ep"), None),
        P("ep", "tp", None),
    )
    return jax.shard_map(
        shards,
        mesh=mesh,
        in_specs=placed,
        out_specs=(P(("dp", "ep"), None, "tp"), P(("dp", "ep"), None), P("ep", "tp", "dp")),
        check_vma=False,
    )
```

```python
import jax
import jax.numpy as jnp
from jax import lax
from jax.sharding import PartitionSpec as P


def shards(grad_out, hidden, gates, expert_ids, down_weight):
    ep_size = lax.axis_size("ep")
    experts_here, hidden_part, model_width = down_weight.shape
    experts_all = ep_size * experts_here
    tok_count, top_count = expert_ids.shape
    capacity = min(tok_count, 3 * tok_count * top_count // (2 * experts_all))
    pair_count = tok_count * top_count
    slot_count = experts_here * capacity
    slots_all = experts_all * capacity
    f32, bf16 = jnp.float32, jnp.bfloat16

    expert_iota = jnp.arange(experts_all, dtype=jnp.int32)
    pair_hot = expert_ids[:, :, None] == expert_iota[None, None, :]
    tok_has = jnp.any(pair_hot, axis=1).astype(bf16)
    tok_iota = lax.optimization_barrier(jnp.arange(tok_count, dtype=jnp.int32))
    earlier = (tok_iota[None, :] < tok_iota[:, None]).astype(bf16)
    before = jnp.dot(earlier, tok_has, preferred_element_type=f32)
    rank_in = jnp.sum(jnp.where(pair_hot, before[:, None, :], 0.0), axis=2).astype(jnp.int32)
    slot_of = (expert_ids * capacity + rank_in).reshape(pair_count)

    slot_iota = lax.optimization_barrier(jnp.arange(slots_all, dtype=jnp.int32))
    sel_pair = (slot_iota[:, None] == slot_of[None, :]).astype(bf16)
    pair_iota = lax.optimization_barrier(jnp.arange(pair_count, dtype=jnp.int32))
    tok_of_pair = (pair_iota[:, None] // top_count == tok_iota[None, :]).astype(bf16)
    sel_tok = jnp.dot(sel_pair, tok_of_pair, preferred_element_type=f32).astype(bf16)

    scaled_pairs = (
        gates.astype(f32)[:, :, None] * hidden.astype(f32)
    ).astype(bf16).reshape(pair_count, hidden_part)
    scaled_rows = jnp.dot(sel_pair, scaled_pairs, preferred_element_type=f32).astype(bf16)
    chosen = jnp.dot(sel_tok, grad_out, preferred_element_type=f32).astype(bf16)

    half_recv = lax.all_to_all(
        chosen.reshape(ep_size, slot_count, grad_out.shape[1]),
        "ep",
        split_axis=0,
        concat_axis=0,
        tiled=True,
    )
    scaled_recv = lax.all_to_all(
        scaled_rows.reshape(ep_size, slot_count, hidden_part), "ep", split_axis=0, concat_axis=0, tiled=True
    )
    dy_recv = lax.all_gather(half_recv, "tp", axis=2, tiled=True)
    dy_slots = dy_recv.reshape(ep_size, experts_here, capacity, model_width)
    scaled_slots = scaled_recv.reshape(ep_size, experts_here, capacity, hidden_part)

    weight_term = jnp.einsum("secf,secd->efd", scaled_slots, dy_slots, preferred_element_type=f32)
    weight_half = weight_term.astype(bf16)
    d_weight = lax.psum_scatter(weight_half, "dp", scatter_dimension=2, tiled=True)

    after = (weight_half[0, 0, 0] * 0).astype(bf16)
    back_proj = jnp.einsum(
        "secd,efd->secf", dy_slots, down_weight + after, preferred_element_type=f32
    )
    got_bp = lax.all_to_all(
        back_proj.astype(bf16).reshape(ep_size, slot_count, hidden_part),
        "ep",
        split_axis=0,
        concat_axis=0,
        tiled=True,
    )
    bp_pairs = jnp.dot(
        sel_pair.T, got_bp.reshape(slots_all, hidden_part), preferred_element_type=f32
    ).reshape(tok_count, top_count, hidden_part)
    d_hidden = (gates.astype(f32)[:, :, None] * bp_pairs).astype(bf16)
    part_dot = jnp.sum(bp_pairs * hidden.astype(f32), axis=2)
    d_gates = lax.psum(part_dot, "tp").astype(bf16)
    return (d_hidden, d_gates, d_weight)


def solution(mesh):
    placed = (
        P(("dp", "ep"), "tp"),
        P(("dp", "ep"), None, "tp"),
        P(("dp", "ep"), None),
        P(("dp", "ep"), None),
        P("ep", "tp", None),
    )
    return jax.shard_map(
        shards,
        mesh=mesh,
        in_specs=placed,
        out_specs=(P(("dp", "ep"), None, "tp"), P(("dp", "ep"), None), P("ep", "tp", "dp")),
        check_vma=False,
    )
```

```python
import jax
import jax.numpy as jnp
from jax import lax
from jax.sharding import PartitionSpec as P


def shards(grad_out, hidden, gates, expert_ids, down_weight):
    ep_size = lax.axis_size("ep")
    experts_here, hidden_part, model_width = down_weight.shape
    experts_all = ep_size * experts_here
    tok_count, top_count = expert_ids.shape
    capacity = min(tok_count, 3 * tok_count * top_count // (2 * experts_all))
    pair_count = tok_count * top_count
    slot_count = experts_here * capacity
    slots_all = experts_all * capacity
    f32, bf16 = jnp.float32, jnp.bfloat16

    expert_iota = jnp.arange(experts_all, dtype=jnp.int32)
    pair_hot = expert_ids[:, :, None] == expert_iota[None, None, :]
    tok_has = jnp.any(pair_hot, axis=1).astype(bf16)
    tok_iota = lax.optimization_barrier(jnp.arange(tok_count, dtype=jnp.int32))
    earlier = (tok_iota[None, :] < tok_iota[:, None]).astype(bf16)
    before = jnp.dot(earlier, tok_has, preferred_element_type=f32)
    rank_in = jnp.sum(jnp.where(pair_hot, before[:, None, :], 0.0), axis=2).astype(jnp.int32)
    slot_of = (expert_ids * capacity + rank_in).reshape(pair_count)

    slot_iota = lax.optimization_barrier(jnp.arange(slots_all, dtype=jnp.int32))
    sel_pair = (slot_iota[:, None] == slot_of[None, :]).astype(bf16)

    hid_rows = jnp.dot(
        sel_pair, hidden.reshape(pair_count, hidden_part), preferred_element_type=f32
    ).astype(bf16)
    gate_rows = jnp.dot(
        sel_pair, gates.reshape(pair_count, 1), preferred_element_type=f32
    ).astype(bf16)

    ids_all = lax.all_gather(expert_ids, "ep")
    own = lax.axis_index("ep") * experts_here + jnp.arange(experts_here, dtype=jnp.int32)
    has_own = jnp.any(ids_all[:, :, :, None] == own[None, None, None, :], axis=2)
    has_own_b = has_own.astype(bf16)
    before_own = jnp.einsum("ts,bsl->btl", earlier, has_own_b, preferred_element_type=f32)
    rank_iota = jnp.arange(capacity, dtype=jnp.int32)
    pick = (
        has_own[:, :, :, None]
        & (before_own.astype(jnp.int32)[:, :, :, None] == rank_iota[None, None, None, :])
    ).astype(bf16)
    chunk = grad_out.shape[1] // 2
    dy_chunks = []
    for part in range(2):
        grad_all = lax.all_gather(grad_out[:, part * chunk : (part + 1) * chunk], "ep")
        picked = (
            jnp.einsum("btlr,btd->blrd", pick, grad_all, preferred_element_type=f32)
            .astype(bf16)
            .reshape(ep_size, slot_count, chunk)
        )
        dy_chunks.append(
            lax.all_gather(picked, "tp", axis=2, tiled=True).reshape(
                ep_size, experts_here, capacity, 2 * chunk
            )
        )
    flat_hid = slot_count * hidden_part
    both = jnp.concatenate(
        [hid_rows.reshape(ep_size, flat_hid), gate_rows.reshape(ep_size, slot_count)], axis=1
    )
    both_recv = lax.all_to_all(both, "ep", split_axis=0, concat_axis=0, tiled=True)
    hid_recv = both_recv[:, :flat_hid]
    gate_recv = both_recv[:, flat_hid:]
    hid_slots = hid_recv.reshape(ep_size, experts_here, capacity, hidden_part)
    gate_slots = gate_recv.reshape(ep_size, experts_here, capacity).astype(f32)

    scaled = (gate_slots[..., None] * hid_slots.astype(f32)).astype(bf16)
    w_parts = down_weight.reshape(experts_here, hidden_part, 2, 2, chunk)
    terms = [
        jnp.einsum("secf,secd->efd", scaled, dy_chunks[part], preferred_element_type=f32)
        .astype(bf16)
        .reshape(experts_here, hidden_part, 2, chunk)
        for part in range(2)
    ]
    weight_half = jnp.stack(terms, axis=3).reshape(experts_here, hidden_part, model_width)
    d_weight = lax.psum_scatter(weight_half, "dp", scatter_dimension=2, tiled=True)

    back_proj = sum(
        jnp.einsum(
            "secd,efd->secf",
            dy_chunks[part],
            w_parts[:, :, :, part, :].reshape(experts_here, hidden_part, 2 * chunk),
            preferred_element_type=f32,
        )
        for part in range(2)
    )
    partial_value = jnp.sum(back_proj * hid_slots.astype(f32), axis=3)
    dot_total = lax.psum(partial_value, "tp")
    send_dh = (
        (gate_slots[..., None] * back_proj)
        .astype(bf16)
        .reshape(ep_size, slot_count, hidden_part)
    )
    send_dg = dot_total.astype(bf16).reshape(ep_size, slot_count)
    back = jnp.concatenate([send_dh.reshape(ep_size, flat_hid), send_dg], axis=1)
    got = lax.all_to_all(back, "ep", split_axis=0, concat_axis=0, tiled=True)
    got_dh = got[:, :flat_hid]
    got_dg = got[:, flat_hid:]
    d_hidden = (
        jnp.dot(sel_pair.T, got_dh.reshape(slots_all, hidden_part), preferred_element_type=f32)
        .astype(bf16)
        .reshape(tok_count, top_count, hidden_part)
    )
    d_gates = (
        jnp.dot(sel_pair.T, got_dg.reshape(slots_all, 1), preferred_element_type=f32)
        .astype(bf16)
        .reshape(tok_count, top_count)
    )
    return (d_hidden, d_gates, d_weight)


def solution(mesh):
    placed = (
        P(("dp", "ep"), "tp"),
        P(("dp", "ep"), None, "tp"),
        P(("dp", "ep"), None),
        P(("dp", "ep"), None),
        P("ep", "tp", None),
    )
    return jax.shard_map(
        shards,
        mesh=mesh,
        in_specs=placed,
        out_specs=(P(("dp", "ep"), None, "tp"), P(("dp", "ep"), None), P("ep", "tp", "dp")),
        check_vma=False,
    )
```
